32 devices in a mesh: vp: 8 (over z, x), op: 4 (over y, core).
Axes of the slice: x: 2, y: 2, z: 4, core: 2. Of those that a mesh axis runs over, the one named last changes fastest.
Arguments:
- amplitudes: bfloat16 [128, 8192], P('op', 'vp'), may hold values from -6 to 6
- driving_term: bfloat16 [128, 8192], P('op', 'vp'), may hold values from -6 to 6
- blocks: bfloat16 [8, 8, 1024, 1024], P('vp', None, 'op'), may hold values from -0.09375 to 0.09375
- block_tile: int32 [8, 8], P('vp'), may hold values from -1 to 7, as said below
- occupied_energy: float32 [128], P('op'), may hold values from 0.5 to 1.5
- virtual_energy: float32 [8192], P('vp'), may hold values from 1 to 3
Outputs:
- amplitudes_next: bfloat16 [128, 8192], P('op', 'vp')
The draws below stay inside these ranges and needn't reach their ends.
Inputs may be any that keep to these rules, and one draw needn't show every extreme that they name: `block_tile`: row a lists slot 0 = a, then distinct tiles within 4 of a in no particular order, then -1 in the unused slots; at least one row uses all 8 slots.
All inputs are finite; a program needn't handle non-finite values.
Results may differ from the reference program's by a relative error of at most 0.0035.
Values may be sent and summed in bfloat16 or wider, within the bound.
A program may use at most 64 MiB of HBM per device.

```python
import math
import jax
import jax.numpy as jnp
from jax import lax

VT = 1024
SLOTS = 8
REACH = 4
ITERS = 2
TILES = 8
NV = 8192
NO = 128


def draw_block_tile(key, part):
    tile_index = jnp.arange(TILES, dtype=jnp.int32)
    key_scores, key_counts = jax.random.split(jax.random.fold_in(key, 11))
    offsets = jnp.concatenate([jnp.arange(-REACH, 0, dtype=jnp.int32), jnp.arange(1, REACH + 1, dtype=jnp.int32)])
    candidates = tile_index[:, None] + offsets[None, :]
    inside = (candidates >= 0) & (candidates < TILES)
    position = jnp.arange(2 * REACH, dtype=jnp.int32)[None, :]
    scores = jax.random.randint(key_scores, (TILES, 2 * REACH), 0, 1 << 20, dtype=jnp.int32) * (2 * REACH) + position
    scores = jnp.where(inside, scores, (1 << 30) + position)
    ordering = jnp.argsort(scores, axis=1)
    picked = jnp.take_along_axis(candidates, ordering, axis=1)
    count_inside = jnp.sum(inside.astype(jnp.int32), axis=1)
    wanted = jax.random.randint(key_counts, (TILES,), 1, SLOTS + 1, dtype=jnp.int32)
    wanted = jnp.where(tile_index == TILES // 2, SLOTS, wanted)
    listed_count = jnp.minimum(wanted, count_inside + 1)
    slot_index = jnp.arange(SLOTS, dtype=jnp.int32)
    filled = jnp.concatenate([tile_index[:, None], picked[:, :SLOTS - 1]], axis=1)
    return jnp.where(slot_index[None, :] < listed_count[:, None], filled, -1).astype(jnp.int32)


def block_levels(own_key, extent, pieces, smallest, top_value):
    def one(axis_at, blocks):
        heights = jax.random.uniform(jax.random.fold_in(jax.random.fold_in(own_key, 6), axis_at), (blocks,), jnp.float32, smallest / len(pieces), top_value / len(pieces))
        return jnp.repeat(jnp.exp(heights), extent[axis_at] // blocks).reshape((-1,) + (1,) * (len(extent) - axis_at - 1))

    loudness = one(*pieces[0])
    for cut in pieces[1:]:
        loudness = loudness * one(*cut)
    return loudness


def normal_values(own_key, shape, spread, bound, shards=(), kind=jnp.bfloat16):
    array = spread * jax.random.normal(own_key, shape, jnp.float32)
    if shards:
        array = array * block_levels(own_key, shape, shards, -0.22, 0.18)
    return jnp.clip(array, -bound, bound).astype(kind)


def setup_inputs(seed: int = 0) -> dict:
    splits = jax.random.split(jax.random.key(seed), 7)
    amplitudes = normal_values(splits[0], (NO, NV), 1.0, 6.0, ((0, 4), (1, 8)))
    driving_term = normal_values(splits[1], (NO, NV), 1.0, 6.0, ((0, 4), (1, 8)))
    blocks = normal_values(splits[2], (TILES, SLOTS, VT, VT), (4 * VT) ** -0.5, 0.09375, ((0, 8), (2, 4)))
    block_tile = draw_block_tile(jax.random.fold_in(splits[6], 71), 0)
    occupied_energy = jnp.clip(jnp.exp(math.log(1.5) - 1.0986123 * jax.random.uniform(splits[4], (NO,), jnp.float32) ** block_levels(splits[4], (NO,), ((0, 4),), -0.2, 0.2)), 0.5, 1.5)
    virtual_energy = jnp.clip(jnp.exp(math.log(3.0) - 1.0986123 * jax.random.uniform(splits[5], (NV,), jnp.float32) ** block_levels(splits[5], (NV,), ((0, 8),), -0.2, 0.2)), 1.0, 3.0)
    return {"amplitudes": amplitudes, "driving_term": driving_term, "blocks": blocks, "block_tile": block_tile, "occupied_energy": occupied_energy, "virtual_energy": virtual_energy}


def reference(amplitudes, driving_term, blocks, block_tile, occupied_energy, virtual_energy):
    inverse = 1.0 / (occupied_energy[:, None] + virtual_energy[None, :])
    current = amplitudes
    for iteration in range(ITERS):
        def one_panel(panel_index):
            sources = block_tile[panel_index]
            total = jnp.zeros((NO, VT), jnp.float32)
            for slot_index in range(SLOTS):
                column_tile = sources[slot_index]
                first_column = (jnp.maximum(column_tile, 0) * VT).astype(jnp.int32)
                source_tile = lax.dynamic_slice_in_dim(current, first_column, VT, 1)
                weights = blocks[panel_index, slot_index]

                def multiply(operands):
                    return jnp.dot(operands[0], operands[1], preferred_element_type=jnp.float32)

                def nothing(operands):
                    return jnp.zeros((NO, VT), jnp.float32)

                product = lax.cond(column_tile >= 0, multiply, nothing, (source_tile, weights))
                total = total + product
            return total

        ladder = lax.map(one_panel, jnp.arange(TILES, dtype=jnp.int32))
        ladder = jnp.transpose(ladder, (1, 0, 2)).reshape(NO, NV)
        current = ((driving_term.astype(jnp.float32) + ladder) * inverse).astype(jnp.bfloat16)
    return current
```

```python
import functools

import jax
import jax.numpy as jnp
from jax import lax
from jax.experimental import pallas as pl
from jax.experimental.pallas import tpu as pltpu
from jax.sharding import PartitionSpec as P

ITERS = 2
REACH = 4
NEAR = 2 * REACH
MESH = pl.DeviceIdType.MESH


def offset_of(i):
    return (i // 2 + 1) * (1 - 2 * (i % 2))


def mirror(i):
    return i + 1 - 2 * (i % 2)


def kernel(
    nv, no, amp_ref, drive_ref, blocks_ref, listed_ref, occ_ref, virt_ref, out_ref,
    blk, own, near, acc, inv, half, summed, rest, cur,
    blk_sem, loc_sem, a_send, a_recv, g_send, g_recv, p_send, p_recv, r_send, r_recv,
):
    v = lax.axis_index("vp")
    o = lax.axis_index("op")
    rows = amp_ref.shape[0]
    slots, width = blk.shape[0], blk.shape[1]
    pair = 2
    groups = no // pair
    side = o % pair
    group = o // pair
    partner = o + 1 - 2 * side

    for k in range(slots):
        pltpu.make_async_copy(blocks_ref.at[0, k], blk.at[k], blk_sem.at[k]).start()

    def exists(d):
        return jnp.logical_and(v + d >= 0, v + d < nv)

    barrier = pltpu.get_barrier_semaphore()
    count = jnp.int32(no - 1)
    for p in range(1, no):
        pl.semaphore_signal(barrier, inc=1, device_id=(v, (o + p) % no), device_id_type=MESH)
    for i in range(NEAR):
        d = offset_of(i)
        valid = exists(d)
        count = count + valid.astype(jnp.int32)

        @pl.when(valid)
        def _():
            pl.semaphore_signal(barrier, inc=1, device_id=(v + d, o), device_id_type=MESH)

    pl.semaphore_wait(barrier, count)

    def spread(it, src, p):
        to = (o + p) % no
        return pltpu.make_async_remote_copy(
            src_ref=src.at[:, pl.ds(pl.multiple_of(to * width, width), width)],
            dst_ref=own.at[it, pl.ds(pl.multiple_of(o * rows, rows), rows), :],
            send_sem=a_send.at[it, p],
            recv_sem=a_recv.at[it, p],
            device_id=(v, to),
            device_id_type=MESH,
        )

    def keep(it, src):
        return pltpu.make_async_copy(
            src.at[:, pl.ds(pl.multiple_of(o * width, width), width)],
            own.at[it, pl.ds(pl.multiple_of(o * rows, rows), rows), :],
            loc_sem.at[it],
        )

    def share(it, i):
        return pltpu.make_async_remote_copy(
            src_ref=own.at[it],
            dst_ref=near.at[it, mirror(i)],
            send_sem=g_send.at[it, i],
            recv_sem=g_recv.at[it, mirror(i)],
            device_id=(v + offset_of(i), o),
            device_id_type=MESH,
        )

    def arrived(it, i):
        return pltpu.make_async_remote_copy(
            src_ref=own.at[it],
            dst_ref=near.at[it, i],
            send_sem=g_send.at[it, i],
            recv_sem=g_recv.at[it, i],
            device_id=(v + offset_of(i), o),
            device_id_type=MESH,
        )

    def fold(it, j):
        return pltpu.make_async_remote_copy(
            src_ref=acc.at[it, pl.ds(pl.multiple_of((j * pair + 1 - side) * rows, rows), rows), :],
            dst_ref=half.at[it, j],
            send_sem=p_send.at[it, j],
            recv_sem=p_recv.at[it, j],
            device_id=(v, partner),
            device_id_type=MESH,
        )

    def settle(it, q):
        to = (group + q) % groups
        return pltpu.make_async_remote_copy(
            src_ref=summed.at[it, q],
            dst_ref=rest.at[it, q],
            send_sem=r_send.at[it, q],
            recv_sem=r_recv.at[it, q],
            device_id=(v, to * pair + side),
            device_id_type=MESH,
        )

    def weight(tile):
        slot = jnp.int32(0)
        hit = jnp.float32(0)
        for k in range(slots):
            same = listed_ref[0, k] == tile
            slot = jnp.where(same, k, slot)
            hit = jnp.where(same, jnp.float32(1), hit)
        return slot, hit

    def product(x, tile):
        slot, hit = weight(tile)
        x = x * jnp.full(x.shape, hit, jnp.float32).astype(x.dtype)
        return jnp.dot(x, blk[slot], preferred_element_type=jnp.float32)

    for it in range(ITERS):
        src = amp_ref if it == 0 else cur
        for p in range(1, no):
            spread(it, src, p).start()
        keep(it, src).start()
        if it == 0:
            eye = lax.broadcasted_iota(jnp.int32, (rows, rows), 0) == lax.broadcasted_iota(
                jnp.int32, (rows, rows), 1
            )
            occ = jnp.sum(
                jnp.where(eye, jnp.broadcast_to(occ_ref[...], (rows, rows)), 0.0),
                axis=1,
                keepdims=True,
            )
            inv[...] = 1.0 / (occ + virt_ref[...])
        keep(it, src).wait()
        for p in range(1, no):
            spread(it, src, p).wait_recv()
        for i in range(NEAR):

            @pl.when(exists(offset_of(i)))
            def _():
                share(it, i).start()

        if it == 0:
            for k in range(slots):
                pltpu.make_async_copy(blocks_ref.at[0, k], blk.at[k], blk_sem.at[k]).wait()
        acc[it] = product(own[it], v)

        def step(i, carry):
            @pl.when(exists(offset_of(i)))
            def _():
                arrived(it, i).wait_recv()
                acc[it] += product(near[it, i], v + offset_of(i))

            return carry

        lax.fori_loop(0, NEAR, step, 0)

        for q in range(1, groups + 1):
            fold(it, (group + q) % groups).start()
        for q in range(1, groups + 1):
            j = (group + q) % groups
            fold(it, j).wait_recv()
            total = acc[it, pl.ds(pl.multiple_of((j * pair + side) * rows, rows), rows), :] + half[it, j]
            if q < groups:
                summed[it, q] = total
                settle(it, q).start()
        for q in range(1, groups):
            settle(it, q).wait_recv()
            total = total + rest[it, q]
        value = ((drive_ref[...].astype(jnp.float32) + total) * inv[...]).astype(jnp.bfloat16)
        if it == ITERS - 1:
            out_ref[...] = value
        else:
            cur[...] = value

    for it in range(ITERS):
        src = amp_ref if it == 0 else cur
        for p in range(1, no):
            spread(it, src, p).wait_send()
        for i in range(NEAR):

            @pl.when(exists(offset_of(i)))
            def _():
                share(it, i).wait_send()

        for j in range(groups):
            fold(it, j).wait_send()
        for q in range(1, groups):
            settle(it, q).wait_send()


def per_device(nv, no, amplitudes, driving_term, blocks, block_tile, occupied_energy, virtual_energy):
    rows, cols = amplitudes.shape
    slots, width = blocks.shape[1], blocks.shape[2]
    groups = no // 2
    dma = pltpu.SemaphoreType.DMA
    vmem = pl.BlockSpec(memory_space=pltpu.VMEM)
    return pl.pallas_call(
        functools.partial(kernel, nv, no),
        out_shape=jax.ShapeDtypeStruct((rows, cols), jnp.bfloat16),
        in_specs=[
            vmem,
            vmem,
            pl.BlockSpec(memory_space=pl.ANY),
            pl.BlockSpec(memory_space=pltpu.SMEM),
            vmem,
            vmem,
        ],
        out_specs=vmem,
        scratch_shapes=[
            pltpu.VMEM((slots, width, cols), jnp.bfloat16),
            pltpu.VMEM((ITERS, no * rows, width), jnp.bfloat16),
            pltpu.VMEM((ITERS, NEAR, no * rows, width), jnp.bfloat16),
            pltpu.VMEM((ITERS, no * rows, cols), jnp.float32),
            pltpu.VMEM((rows, cols), jnp.float32),
            pltpu.VMEM((ITERS, groups, rows, cols), jnp.float32),
            pltpu.VMEM((ITERS, groups, rows, cols), jnp.float32),
            pltpu.VMEM((ITERS, groups, rows, cols), jnp.float32),
            pltpu.VMEM((rows, cols), jnp.bfloat16),
            dma((slots,)),
            dma((ITERS,)),
            dma((ITERS, no)),
            dma((ITERS, no)),
            dma((ITERS, NEAR)),
            dma((ITERS, NEAR)),
            dma((ITERS, groups)),
            dma((ITERS, groups)),
            dma((ITERS, groups)),
            dma((ITERS, groups)),
        ],
        compiler_params=pltpu.CompilerParams(
            collective_id=0, has_side_effects=True, vmem_limit_bytes=40 << 20
        ),
    )(
        amplitudes,
        driving_term,
        blocks,
        block_tile,
        occupied_energy.reshape(1, rows),
        virtual_energy.reshape(1, cols),
    )


def solution(mesh):
    in_specs = (
        P("op", "vp"),
        P("op", "vp"),
        P("vp", None, "op", None),
        P("vp", None),
        P("op"),
        P("vp"),
    )
    return jax.shard_map(
        functools.partial(per_device, mesh.shape["vp"], mesh.shape["op"]),
        mesh=mesh,
        in_specs=in_specs,
        out_specs=P("op", "vp"),
        check_vma=False,
    )
```

```python
import functools

import jax
import jax.numpy as jnp
from jax import lax
from jax.experimental import pallas as pl
from jax.experimental.pallas import tpu as pltpu
from jax.sharding import PartitionSpec as P

ITERS = 2
REACH = 4
NEAR = 2 * REACH
MESH = pl.DeviceIdType.MESH


def offset_of(i):
    return (i // 2 + 1) * (1 - 2 * (i % 2))


def mirror(i):
    return i + 1 - 2 * (i % 2)


def kernel(
    nv, no, amp_ref, drive_ref, blocks_ref, listed_ref, occ_ref, virt_ref, out_ref,
    blk, own, near, acc, drive_rows, drive_cols, occ, virt, inv_rows, inv_cols,
    half_cols, summed_cols, rest_cols, half_rows, summed_rows, rest_rows,
    blk_sem, in_sem, loc_sem, a_send, a_recv, g_send, g_recv, p_send, p_recv, r_send, r_recv,
):
    v = lax.axis_index("vp")
    o = lax.axis_index("op")
    rows = amp_ref.shape[0]
    slots, width = blk.shape[0], blk.shape[1]
    pair = 2
    groups = no // pair
    side = o % pair
    group = o // pair
    partner = o + 1 - 2 * side

    def load_block(k):
        return pltpu.make_async_copy(blocks_ref.at[0, k], blk.at[k], blk_sem.at[k])

    loads = (
        pltpu.make_async_copy(virt_ref, virt, in_sem.at[0]),
        pltpu.make_async_copy(drive_ref, drive_rows, in_sem.at[1]),
    )
    for load in loads:
        load.start()
    for k in range(slots):
        load_block(k).start()

    def exists(d):
        return jnp.logical_and(v + d >= 0, v + d < nv)

    barrier = pltpu.get_barrier_semaphore()
    count = jnp.int32(no - 1)
    for p in range(1, no):
        pl.semaphore_signal(barrier, inc=1, device_id=(v, (o + p) % no), device_id_type=MESH)
    for i in range(NEAR):
        d = offset_of(i)
        valid = exists(d)
        count = count + valid.astype(jnp.int32)

        @pl.when(valid)
        def _():
            pl.semaphore_signal(barrier, inc=1, device_id=(v + d, o), device_id_type=MESH)

    pl.semaphore_wait(barrier, count)

    def my_rows(ref):
        return ref.at[pl.ds(pl.multiple_of(o * rows, rows), rows), :]

    def columns(ref, owner):
        return ref.at[:, pl.ds(pl.multiple_of(owner * width, width), width)]

    def pieces(to):
        return (
            (columns(amp_ref, to), my_rows(own.at[0])),
            (columns(drive_ref, to), my_rows(drive_cols)),
            (occ_ref, occ.at[o]),
        )

    def spread(n, p):
        to = (o + p) % no
        piece = pieces(to)[n]
        return pltpu.make_async_remote_copy(
            src_ref=piece[0],
            dst_ref=piece[1],
            send_sem=a_send.at[n, p],
            recv_sem=a_recv.at[n, p],
            device_id=(v, to),
            device_id_type=MESH,
        )

    def keep(n):
        piece = pieces(o)[n]
        return pltpu.make_async_copy(piece[0], piece[1], loc_sem.at[n])

    def share(it, i):
        return pltpu.make_async_remote_copy(
            src_ref=own.at[it],
            dst_ref=near.at[it, mirror(i)],
            send_sem=g_send.at[it, i],
            recv_sem=g_recv.at[it, mirror(i)],
            device_id=(v + offset_of(i), o),
            device_id_type=MESH,
        )

    def arrived(it, i):
        return pltpu.make_async_remote_copy(
            src_ref=own.at[it],
            dst_ref=near.at[it, i],
            send_sem=g_send.at[it, i],
            recv_sem=g_recv.at[it, i],
            device_id=(v + offset_of(i), o),
            device_id_type=MESH,
        )

    half = (half_cols, half_rows)
    summed = (summed_cols, summed_rows)
    rest = (rest_cols, rest_rows)

    def part(it, owner):
        if it < ITERS - 1:
            return acc.at[it, :, pl.ds(pl.multiple_of(owner * width, width), width)]
        return acc.at[it, pl.ds(pl.multiple_of(owner * rows, rows), rows), :]

    def fold(it, j):
        return pltpu.make_async_remote_copy(
            src_ref=part(it, j * pair + 1 - side),
            dst_ref=half[it].at[j],
            send_sem=p_send.at[it, j],
            recv_sem=p_recv.at[it, j],
            device_id=(v, partner),
            device_id_type=MESH,
        )

    def settle(it, q):
        to = (group + q) % groups
        return pltpu.make_async_remote_copy(
            src_ref=summed[it].at[q],
            dst_ref=rest[it].at[q],
            send_sem=r_send.at[it, q],
            recv_sem=r_recv.at[it, q],
            device_id=(v, to * pair + side),
            device_id_type=MESH,
        )

    def weight(tile):
        slot = jnp.int32(0)
        hit = jnp.float32(0)
        for k in range(slots):
            same = listed_ref[0, k] == tile
            slot = jnp.where(same, k, slot)
            hit = jnp.where(same, jnp.float32(1), hit)
        return slot, hit

    def product(x, tile):
        slot, hit = weight(tile)
        x = x * jnp.full(x.shape, hit, jnp.float32).astype(x.dtype)
        return jnp.dot(x, blk[slot], preferred_element_type=jnp.float32)

    def inverse(i, columns_of):
        eye = lax.broadcasted_iota(jnp.int32, (rows, rows), 0) == lax.broadcasted_iota(
            jnp.int32, (rows, rows), 1
        )
        energy = jnp.sum(
            jnp.where(eye, jnp.broadcast_to(occ[i], (rows, rows)), 0.0), axis=1, keepdims=True
        )
        return 1.0 / (energy + columns_of)

    for n in range(3):
        for p in range(1, no):
            spread(n, p).start()
        keep(n).start()
    keep(0).wait()
    for p in range(1, no):
        spread(0, p).wait_recv()

    for it in range(ITERS):
        for i in range(NEAR):

            @pl.when(exists(offset_of(i)))
            def _():
                share(it, i).start()

        if it == 0:
            for load in loads:
                load.wait()
            for n in range(1, 3):
                keep(n).wait()
                for p in range(1, no):
                    spread(n, p).wait_recv()
            mine = virt[:, pl.ds(pl.multiple_of(o * width, width), width)]
            for i in range(no):
                inv_cols[i * rows : (i + 1) * rows, :] = inverse(i, mine)
            inv_rows[...] = inverse(o, virt[...])
            for k in range(slots):
                load_block(k).wait()
        acc[it] = product(own[it], v)

        def step(i, carry):
            @pl.when(exists(offset_of(i)))
            def _():
                arrived(it, i).wait_recv()
                acc[it] += product(near[it, i], v + offset_of(i))

            return carry

        lax.fori_loop(0, NEAR, step, 0)

        for q in range(1, groups + 1):
            fold(it, (group + q) % groups).start()
        for q in range(1, groups + 1):
            j = (group + q) % groups
            fold(it, j).wait_recv()
            total = part(it, j * pair + side)[...] + half[it][j]
            if q < groups:
                summed[it][q] = total
                settle(it, q).start()
        for q in range(1, groups):
            settle(it, q).wait_recv()
            total = total + rest[it][q]
        if it == ITERS - 1:
            value = (drive_rows[...].astype(jnp.float32) + total) * inv_rows[...]
            out_ref[...] = value.astype(jnp.bfloat16)
        else:
            value = (drive_cols[...].astype(jnp.float32) + total) * inv_cols[...]
            own[it + 1] = value.astype(jnp.bfloat16)

    for n in range(3):
        for p in range(1, no):
            spread(n, p).wait_send()
    for it in range(ITERS):
        for i in range(NEAR):

            @pl.when(exists(offset_of(i)))
            def _():
                share(it, i).wait_send()

        for j in range(groups):
            fold(it, j).wait_send()
        for q in range(1, groups):
            settle(it, q).wait_send()


def per_device(nv, no, amplitudes, driving_term, blocks, block_tile, occupied_energy, virtual_energy):
    rows, cols = amplitudes.shape
    slots, width = blocks.shape[1], blocks.shape[2]
    groups = no // 2
    dma = pltpu.SemaphoreType.DMA
    hbm = pl.BlockSpec(memory_space=pltpu.HBM)
    return pl.pallas_call(
        functools.partial(kernel, nv, no),
        out_shape=jax.ShapeDtypeStruct((rows, cols), jnp.bfloat16),
        in_specs=[hbm, hbm, hbm, pl.BlockSpec(memory_space=pltpu.SMEM), hbm, hbm],
        out_specs=pl.BlockSpec(memory_space=pltpu.VMEM),
        scratch_shapes=[
            pltpu.VMEM((slots, width, cols), jnp.bfloat16),
            pltpu.VMEM((ITERS, no * rows, width), jnp.bfloat16),
            pltpu.VMEM((ITERS, NEAR, no * rows, width), jnp.bfloat16),
            pltpu.VMEM((ITERS, no * rows, cols), jnp.float32),
            pltpu.VMEM((rows, cols), jnp.bfloat16),
            pltpu.VMEM((no * rows, width), jnp.bfloat16),
            pltpu.VMEM((no, 1, rows), jnp.float32),
            pltpu.VMEM((1, cols), jnp.float32),
            pltpu.VMEM((rows, cols), jnp.float32),
            pltpu.VMEM((no * rows, width), jnp.float32),
        ]
        + [pltpu.VMEM((groups, no * rows, width), jnp.float32)] * 3
        + [pltpu.VMEM((groups, rows, cols), jnp.float32)] * 3
        + [
            dma((slots,)),
            dma((2,)),
            dma((3,)),
            dma((3, no)),
            dma((3, no)),
            dma((ITERS, NEAR)),
            dma((ITERS, NEAR)),
            dma((ITERS, groups)),
            dma((ITERS, groups)),
            dma((ITERS, groups)),
            dma((ITERS, groups)),
        ],
        compiler_params=pltpu.CompilerParams(
            collective_id=0, has_side_effects=True, vmem_limit_bytes=60 << 20
        ),
    )(
        amplitudes,
        driving_term,
        blocks,
        block_tile,
        occupied_energy.reshape(1, rows),
        virtual_energy.reshape(1, cols),
    )


def solution(mesh):
    in_specs = (
        P("op", "vp"),
        P("op", "vp"),
        P("vp", None, "op", None),
        P("vp", None),
        P("op"),
        P("vp"),
    )
    return jax.shard_map(
        functools.partial(per_device, mesh.shape["vp"], mesh.shape["op"]),
        mesh=mesh,
        in_specs=in_specs,
        out_specs=P("op", "vp"),
        check_vma=False,
    )
```

```python
import functools

import jax
import jax.numpy as jnp
from jax import lax
from jax.experimental import pallas as pl
from jax.experimental.pallas import tpu as pltpu
from jax.sharding import PartitionSpec as P

ITERS = 2
REACH = 4
NEAR = 2 * REACH
CUT = 5
MESH = pl.DeviceIdType.MESH


def index_of(e):
    return 2 * (abs(e) - 1) + jnp.int32(e < 0)


def kernel(
    nv, no, amp_ref, drive_ref, blocks_ref, listed_ref, occ_ref, virt_ref, out_ref,
    blk, own, near, acc, drive_rows, drive_cols, amp, occ, virt, inv_rows, inv_cols,
    half_cols, summed_cols, rest_cols, half_rows, summed_rows, rest_rows,
    blk_sem, in_sem, loc_sem, a_send, a_recv, g_send, g_recv, f_send, f_recv, h_send, h_recv, p_send, p_recv, r_send, r_recv,
):
    v = lax.axis_index("vp")
    o = lax.axis_index("op")
    rows = amp_ref.shape[0]
    slots, width = blk.shape[0], blk.shape[1]
    pair = 2
    groups = no // pair
    side = o % pair
    group = o // pair
    partner = o + 1 - 2 * side
    total_rows = no * rows
    w = 1 - 2 * (v % 2)
    direct = (w, 2, -2, 4 * w, -4 * w)
    passed = (2, -2, 4 * w)
    cut = total_rows * CUT // 8 // 16 * 16

    def load_block(k):
        return pltpu.make_async_copy(blocks_ref.at[0, k], blk.at[k], blk_sem.at[k])

    loads = (
        pltpu.make_async_copy(virt_ref, virt, in_sem.at[0]),
        pltpu.make_async_copy(drive_ref, drive_rows, in_sem.at[1]),
    )
    stage = pltpu.make_async_copy(amp_ref, amp, in_sem.at[2])
    stage.start()
    for load in loads:
        load.start()
    for k in range(slots):
        load_block(k).start()

    def exists(d):
        return jnp.logical_and(v + d >= 0, v + d < nv)

    barrier = pltpu.get_barrier_semaphore()
    count = jnp.int32(no - 1)
    for p in range(1, no):
        pl.semaphore_signal(barrier, inc=1, device_id=(v, (o + p) % no), device_id_type=MESH)
    for e in direct:
        valid = exists(e)
        count = count + valid.astype(jnp.int32)

        @pl.when(valid)
        def _():
            pl.semaphore_signal(barrier, inc=1, device_id=(v + e, o), device_id_type=MESH)

    pl.semaphore_wait(barrier, count)

    def my_rows(ref):
        return ref.at[pl.ds(pl.multiple_of(o * rows, rows), rows), :]

    def columns(ref, owner):
        return ref.at[:, pl.ds(pl.multiple_of(owner * width, width), width)]

    def pieces(to):
        return (
            (columns(amp, to), my_rows(own.at[0])),
            (columns(drive_ref, to), my_rows(drive_cols)),
            (occ_ref, occ.at[o]),
        )

    def spread(n, p):
        to = (o + p) % no
        piece = pieces(to)[n]
        return pltpu.make_async_remote_copy(
            src_ref=piece[0],
            dst_ref=piece[1],
            send_sem=a_send.at[n, p],
            recv_sem=a_recv.at[n, p],
            device_id=(v, to),
            device_id_type=MESH,
        )

    def keep(n):
        piece = pieces(o)[n]
        return pltpu.make_async_copy(piece[0], piece[1], loc_sem.at[n])

    def give(it, e, slot):
        return pltpu.make_async_remote_copy(
            src_ref=own.at[it],
            dst_ref=near.at[it, slot],
            send_sem=g_send.at[it, index_of(e)],
            recv_sem=g_recv.at[it, slot],
            device_id=(v + e, o),
            device_id_type=MESH,
        )

    def share(it, e):
        return give(it, e, index_of(-e))

    def arrived(it, e):
        return give(it, e, index_of(e))

    def span(n):
        return pl.ds(0, total_rows if n == 2 else cut)

    def across(it, n, slot):
        return pltpu.make_async_remote_copy(
            src_ref=near.at[it, index_of(passed[n]), span(n), :],
            dst_ref=near.at[it, slot, span(n), :],
            send_sem=f_send.at[it, n],
            recv_sem=f_recv.at[it, n],
            device_id=(v + w, o),
            device_id_type=MESH,
        )

    def along(it, n, m, slot):
        low = pl.ds(cut, total_rows - cut)
        return pltpu.make_async_remote_copy(
            src_ref=near.at[it, index_of(w), low, :],
            dst_ref=near.at[it, slot, low, :],
            send_sem=h_send.at[it, n],
            recv_sem=h_recv.at[it, m],
            device_id=(v + passed[n], o),
            device_id_type=MESH,
        )

    half = (half_cols, half_rows)
    summed = (summed_cols, summed_rows)
    rest = (rest_cols, rest_rows)

    def part(it, owner):
        if it < ITERS - 1:
            return acc.at[it, :, pl.ds(pl.multiple_of(owner * width, width), width)]
        return acc.at[it, pl.ds(pl.multiple_of(owner * rows, rows), rows), :]

    def fold(it, j):
        return pltpu.make_async_remote_copy(
            src_ref=part(it, j * pair + 1 - side),
            dst_ref=half[it].at[j],
            send_sem=p_send.at[it, j],
            recv_sem=p_recv.at[it, j],
            device_id=(v, partner),
            device_id_type=MESH,
        )

    def settle(it, q):
        to = (group + q) % groups
        return pltpu.make_async_remote_copy(
            src_ref=summed[it].at[q],
            dst_ref=rest[it].at[q],
            send_sem=r_send.at[it, q],
            recv_sem=r_recv.at[it, q],
            device_id=(v, to * pair + side),
            device_id_type=MESH,
        )

    def weight(tile):
        slot = jnp.int32(0)
        hit = jnp.float32(0)
        for k in range(slots):
            same = listed_ref[0, k] == tile
            slot = jnp.where(same, k, slot)
            hit = jnp.where(same, jnp.float32(1), hit)
        return slot, hit

    def product(x, tile):
        slot, hit = weight(tile)
        x = x * jnp.full(x.shape, hit, jnp.float32).astype(x.dtype)
        return jnp.dot(x, blk[slot], preferred_element_type=jnp.float32)

    def inverse(i, columns_of):
        eye = lax.broadcasted_iota(jnp.int32, (rows, rows), 0) == lax.broadcasted_iota(
            jnp.int32, (rows, rows), 1
        )
        energy = jnp.sum(
            jnp.where(eye, jnp.broadcast_to(occ[i], (rows, rows)), 0.0), axis=1, keepdims=True
        )
        return 1.0 / (energy + columns_of)

    stage.wait()
    for n in range(3):
        for p in range(1, no):
            spread(n, p).start()
        keep(n).start()
    keep(0).wait()
    for p in range(1, no):
        spread(0, p).wait_recv()

    for it in range(ITERS):
        for e in direct:

            @pl.when(exists(e))
            def _():
                share(it, e).start()

        if it == 0:
            for load in loads:
                load.wait()
            for n in range(1, 3):
                keep(n).wait()
                for p in range(1, no):
                    spread(n, p).wait_recv()
            mine = virt[:, pl.ds(pl.multiple_of(o * width, width), width)]
            for i in range(no):
                inv_cols[i * rows : (i + 1) * rows, :] = inverse(i, mine)
            inv_rows[...] = inverse(o, virt[...])
            for k in range(slots):
                load_block(k).wait()
        acc[it] = product(own[it], v)

        def add(e):
            acc[it] += product(near[it, index_of(e)], v + e)

        arrived(it, w).wait_recv()
        for n in range(2):

            @pl.when(exists(passed[n]))
            def _():
                along(it, n, 1 - n, index_of(w - passed[n])).start()

        add(w)
        for n in range(3):

            @pl.when(exists(passed[n]))
            def _():
                arrived(it, passed[n]).wait_recv()
                across(it, n, index_of(passed[n] - w)).start()
                add(passed[n])

        @pl.when(exists(-4 * w))
        def _():
            arrived(it, -4 * w).wait_recv()
            add(-4 * w)

        for n in range(3):
            far = -3 * w if n == 2 else passed[n] + w

            @pl.when(exists(far))
            def _():
                across(it, n, index_of(far)).wait_recv()
                if n < 2:
                    along(it, n, n, index_of(far)).wait_recv()
                add(far)
        for q in range(1, groups + 1):
            fold(it, (group + q) % groups).start()
        for q in range(1, groups + 1):
            j = (group + q) % groups
            fold(it, j).wait_recv()
            total = part(it, j * pair + side)[...] + half[it][j]
            if q < groups:
                summed[it][q] = total.astype(jnp.bfloat16)
                settle(it, q).start()
        for q in range(1, groups):
            settle(it, q).wait_recv()
            total = total + rest[it][q].astype(jnp.float32)
        if it == ITERS - 1:
            value = (drive_rows[...].astype(jnp.float32) + total) * inv_rows[...]
            out_ref[...] = value.astype(jnp.bfloat16)
        else:
            value = (drive_cols[...].astype(jnp.float32) + total) * inv_cols[...]
            own[it + 1] = value.astype(jnp.bfloat16)

    for n in range(3):
        for p in range(1, no):
            spread(n, p).wait_send()
    for it in range(ITERS):
        for e in direct:

            @pl.when(exists(e))
            def _():
                share(it, e).wait_send()

        for n in range(3):

            @pl.when(exists(passed[n]))
            def _():
                across(it, n, index_of(passed[n] - w)).wait_send()
                if n < 2:
                    along(it, n, 1 - n, index_of(w - passed[n])).wait_send()

        for j in range(groups):
            fold(it, j).wait_send()
        for q in range(1, groups):
            settle(it, q).wait_send()


def per_device(nv, no, amplitudes, driving_term, blocks, block_tile, occupied_energy, virtual_energy):
    rows, cols = amplitudes.shape
    slots, width = blocks.shape[1], blocks.shape[2]
    groups = no // 2
    dma = pltpu.SemaphoreType.DMA
    settled = (jnp.float32, jnp.bfloat16, jnp.bfloat16)
    hbm = pl.BlockSpec(memory_space=pltpu.HBM)
    return pl.pallas_call(
        functools.partial(kernel, nv, no),
        out_shape=jax.ShapeDtypeStruct((rows, cols), jnp.bfloat16),
        in_specs=[hbm, hbm, hbm, pl.BlockSpec(memory_space=pltpu.SMEM), hbm, hbm],
        out_specs=pl.BlockSpec(memory_space=pltpu.VMEM),
        scratch_shapes=[
            pltpu.VMEM((slots, width, cols), jnp.bfloat16),
            pltpu.VMEM((ITERS, no * rows, width), jnp.bfloat16),
            pltpu.VMEM((ITERS, NEAR, no * rows, width), jnp.bfloat16),
            pltpu.VMEM((ITERS, no * rows, cols), jnp.float32),
            pltpu.VMEM((rows, cols), jnp.bfloat16),
            pltpu.VMEM((no * rows, width), jnp.bfloat16),
            pltpu.VMEM((rows, cols), jnp.bfloat16),
            pltpu.VMEM((no, 1, rows), jnp.float32),
            pltpu.VMEM((1, cols), jnp.float32),
            pltpu.VMEM((rows, cols), jnp.float32),
            pltpu.VMEM((no * rows, width), jnp.float32),
        ]
        + [pltpu.VMEM((groups, no * rows, width), t) for t in settled]
        + [pltpu.VMEM((groups, rows, cols), t) for t in settled]
        + [
            dma((slots,)),
            dma((3,)),
            dma((3,)),
            dma((3, no)),
            dma((3, no)),
            dma((ITERS, NEAR)),
            dma((ITERS, NEAR)),
            dma((ITERS, 3)),
            dma((ITERS, 3)),
            dma((ITERS, 2)),
            dma((ITERS, 2)),
            dma((ITERS, groups)),
            dma((ITERS, groups)),
            dma((ITERS, groups)),
            dma((ITERS, groups)),
        ],
        compiler_params=pltpu.CompilerParams(
            collective_id=0, has_side_effects=True, vmem_limit_bytes=60 << 20
        ),
    )(
        amplitudes,
        driving_term,
        blocks,
        block_tile,
        occupied_energy.reshape(1, rows),
        virtual_energy.reshape(1, cols),
    )


def solution(mesh):
    in_specs = (
        P("op", "vp"),
        P("op", "vp"),
        P("vp", None, "op", None),
        P("vp", None),
        P("op"),
        P("vp"),
    )
    return jax.shard_map(
        functools.partial(per_device, mesh.shape["vp"], mesh.shape["op"]),
        mesh=mesh,
        in_specs=in_specs,
        out_specs=P("op", "vp"),
        check_vma=False,
    )
```
